32 devices in a mesh: dp: 4 (over x, core), expert: 8 (over z, y).
Axes of the slice: x: 2, y: 2, z: 4, core: 2. Of those that a mesh axis runs over, the one named last changes fastest.
Arguments:
- tokens: bfloat16 [4096, 4096], P(('dp', 'expert')), may hold values from -6 to 6
- moe_gain: float32 [4096], replicated, may hold values from 0.5 to 1.5
- route_ids: int32 [4096, 2], P(('dp', 'expert')), may hold values from 0 to 7, all different within a row; in each aligned block of 128 rows (0 to 127, 128 to 255, ...) at most 40 rows name the same one
- route_gates: float32 [4096, 2], P(('dp', 'expert')), may hold values from 0.1 to 1
- gate_halves: bfloat16 [32, 4096, 384], P(('dp', 'expert')), may hold values from -0.09375 to 0.09375
- up_halves: bfloat16 [32, 4096, 384], P(('dp', 'expert')), may hold values from -0.09375 to 0.09375
- down_halves: bfloat16 [32, 384, 4096], P(('dp', 'expert')), may hold values from -0.15625 to 0.15625
- head_gain: float32 [4096], replicated, may hold values from 0.5 to 1.5
- head_weight: bfloat16 [4096, 512], P('expert'), may hold values from -0.09375 to 0.09375
- query_scale: float32 [512], replicated, may hold values from 1 to 4
- members: int32 [4096], P(('dp', 'expert')), may hold values from 0 to 4095, as said below
- click_targets: int32 [64, 8], P(('dp', 'expert')), may hold values from 0 to 55
Outputs:
- layer_out: bfloat16 [4096, 4096], P(('dp', 'expert'))
- click_logits: float32 [64, 8, 56], P(('dp', 'expert'))
- click_loss: float32 [64, 8], P(('dp', 'expert'))
The draws below stay inside these ranges and needn't reach their ends.
Inputs may be any that keep to these rules, and one draw needn't show every extreme that they name: `route_ids`: in the 128 rows of one device no expert id is named by more than 40 routes, a bound that some block reaches; the 2 ids of a row differ. `members`: for each index of dp, the 1024 entries of that dp index are a permutation of the tokens of that dp index; every device's 128 entries name exactly 16 tokens of each device of its dp index.
All inputs are finite; a program needn't handle non-finite values.
Results may differ from the reference program's by a relative error of at most 0.0081.
Values may be sent and summed in bfloat16 or wider, within the bound.
A program may use at most 192 MiB of HBM per device.

```python
import math
import jax
import jax.numpy as jnp
import numpy as np
from jax import lax

D = 4096
FF = 1536
TOPK = 2
DH = 512
PATCHES = 56
QUERIES = 8
TOK_DEV = 128
EXPERTS = 8
CAP = 40
TOKENS = 4096
SHOTS = 64
N_DP = 4
N_EXPERT = 8


def draw_members(key, part):
    row_length = N_EXPERT * TOK_DEV
    per_pair = TOK_DEV // N_EXPERT

    def one_row(row_key, row_id):
        split_keys = jax.random.split(row_key, 2 * N_EXPERT)
        orders = jax.vmap(lambda order_key: jax.random.permutation(order_key, TOK_DEV))(split_keys[:N_EXPERT])
        groups = orders.astype(jnp.int32).reshape(N_EXPERT, N_EXPERT, per_pair)
        source_ids = jnp.arange(N_EXPERT, dtype=jnp.int32)[:, None, None]
        within = source_ids * TOK_DEV + groups
        by_owner = jnp.transpose(within, (1, 0, 2)).reshape(N_EXPERT, TOK_DEV)
        shuffled = jax.vmap(lambda order_key, listed: jax.random.permutation(order_key, listed))(split_keys[N_EXPERT:], by_owner)
        return (row_id * row_length + shuffled.reshape(-1)).astype(jnp.int32)
    rows_all = jax.vmap(one_row)(jax.random.split(key, N_DP), jnp.arange(N_DP, dtype=jnp.int32))
    return rows_all.reshape(-1).astype(jnp.int32)


def with_ends(drawn, key, least, top_value):
    index_at = [jax.random.randint(jax.random.fold_in(key, axis), (), 0, length) for axis, length in enumerate(drawn.shape)]
    main_axis = drawn.shape.index(max(drawn.shape))
    next_to = index_at[:main_axis] + [(index_at[main_axis] + 1) % drawn.shape[main_axis]] + index_at[main_axis + 1:]
    return drawn.at[tuple(index_at)].set(least).at[tuple(next_to)].set(top_value)


def steps_of(key, dims, cuts, low, largest):
    level, own = 1.0, jax.random.fold_in(key, 6)
    for position, shards_of in cuts:
        heights = jnp.exp(jax.random.uniform(jax.random.fold_in(own, position), (shards_of,), jnp.float32, low / len(cuts), largest / len(cuts)))
        level = level * jnp.repeat(heights, dims[position] // shards_of).reshape([-1 if axis == position else 1 for axis in range(len(dims))])
    return level


def deal_out(stream_key, own, number, rows, amount, top, most, skew):
    order = jax.random.permutation(stream_key, amount)
    heavy_load, ordinary = shares(amount, rows * top, most, skew, True), shares(amount, rows * top, most, skew, False)
    places = jnp.arange(amount)

    def named(lengths, turn):
        used = int((lengths > 0).sum())
        fixed = max(1, used // 4)
        moved = fixed + (places - fixed + turn * (used - fixed)) % max(1, amount - fixed)
        return jnp.zeros((amount,), jnp.int32).at[order[jnp.where(places < fixed, places, moved)]].set(jnp.asarray(lengths, jnp.int32))

    lengths = jnp.where(number % 4 == 0, named(heavy_load, number // 4), named(ordinary, number - number // 4 - 1))
    mixed = jax.random.permutation(jax.random.fold_in(own, 3), amount)
    source_of, taker = mixed[0:amount // 2 * 2:2], mixed[1:amount // 2 * 2:2]
    slack = jnp.minimum(lengths[source_of] - 1, most - lengths[taker]) // 2
    slack = jnp.where((source_of == order[0]) | (taker == order[0]) | (lengths[taker] == 0), 0, jnp.maximum(slack, 0))
    moved = jax.random.randint(jax.random.fold_in(own, 4), (amount // 2,), 0, 1 << 20) % (slack + 1)
    lengths = lengths.at[source_of].add(-moved).at[taker].add(moved)
    items = jnp.searchsorted(jnp.cumsum(lengths), jnp.arange(rows * top), side="right").astype(jnp.int32)
    table = items.reshape(top, rows).T
    table = table[jax.random.permutation(jax.random.fold_in(own, 1), rows)]
    turn = jax.random.randint(jax.random.fold_in(own, 2), (rows, 1), 0, top)
    return jnp.take_along_axis(table, (jnp.arange(top)[None, :] + turn) % top, axis=1)


def shares(count, total, bound, skew, full):
    loads = [(1 << 20) // math.isqrt(rank ** skew) + 1 for rank in range(1, count + 1)]
    largest = bound if full else min(bound, max(-(-total // count), total * loads[0] // sum(loads)))
    least = 1 if total - largest >= count - 1 else 0
    given, spare = [largest] + [least] * (count - 1), total - largest - least * (count - 1)
    while spare > 0:
        candidates = [i for i in range(1, count) if given[i] < largest] or [i for i in range(1, count) if given[i] < bound]
        mass, remaining = sum([loads[i] for i in candidates]), spare
        for i in candidates:
            extra = min(bound - given[i], max(1, remaining * loads[i] // mass), spare)
            given[i] = given[i] + extra
            spare = spare - extra
    return np.array(given)


def gaussian(stream_key, dims, spread, reach, shards=(), kind=jnp.bfloat16):
    result = spread * jax.random.normal(stream_key, dims, jnp.float32)
    if shards:
        result = result * steps_of(stream_key, dims, shards, -0.22, 0.18)
    return jnp.clip(result, -reach, reach).astype(kind)


def setup_inputs(seed: int = 0) -> dict:
    streams_of = jax.random.split(jax.random.key(seed), 13)
    tokens = gaussian(streams_of[0], (TOKENS, D), 1.0, 6.0, ((0, 32),))
    moe_gain = jnp.clip(1.0 + 0.1 * jax.random.normal(streams_of[1], (D,), jnp.float32), 0.5, 1.5)
    route_ids_keys = jax.random.split(jax.random.fold_in(streams_of[2], 1), TOKENS // TOK_DEV)
    route_ids_turns = jax.random.permutation(jax.random.fold_in(streams_of[2], 3), TOKENS // TOK_DEV)
    route_ids = jax.vmap(lambda own, number: deal_out(jax.random.fold_in(streams_of[2], 2), own, number, TOK_DEV, EXPERTS, TOPK, CAP, 2))(route_ids_keys, route_ids_turns).reshape((TOKENS, TOPK))
    route_gates = jnp.clip(jnp.exp(math.log(1.0) - 2.3025851 * jax.random.uniform(streams_of[3], (TOKENS, TOPK), jnp.float32) ** steps_of(streams_of[3], (TOKENS, TOPK), ((0, 32),), -0.2, 0.2)), 0.1, 1.0)
    gate_halves = gaussian(streams_of[4], (4 * EXPERTS, D, FF // 4), D ** -0.5, 0.09375, ((0, 32),))
    up_halves = gaussian(streams_of[5], (4 * EXPERTS, D, FF // 4), D ** -0.5, 0.09375, ((0, 32),))
    down_halves = gaussian(streams_of[6], (4 * EXPERTS, FF // 4, D), FF ** -0.5, 0.15625, ((0, 32),))
    head_gain = jnp.clip(1.0 + 0.1 * jax.random.normal(streams_of[7], (D,), jnp.float32), 0.5, 1.5)
    head_weight = gaussian(streams_of[8], (D, DH), D ** -0.5, 0.09375, ((0, 8),))
    query_scale = jnp.clip(jnp.exp(jax.random.uniform(streams_of[9], (DH,), jnp.float32, math.log(1.0), math.log(4.0))), 1.0, 4.0)
    members = draw_members(jax.random.fold_in(streams_of[12], 71), 0)
    click_targets = with_ends(jax.random.randint(streams_of[11], (SHOTS, QUERIES), 0, PATCHES), jax.random.fold_in(streams_of[11], 1), 0, PATCHES - 1).astype(jnp.int32)
    return dict(tokens=tokens, moe_gain=moe_gain, route_ids=route_ids, route_gates=route_gates, gate_halves=gate_halves, up_halves=up_halves, down_halves=down_halves, head_gain=head_gain, head_weight=head_weight, query_scale=query_scale, members=members, click_targets=click_targets)


def rms_scale(values, gains):
    mean_square = lax.optimization_barrier(jnp.mean(values * values, axis=-1, keepdims=True))
    return values * lax.rsqrt(mean_square + 1e-06) * gains

def reference(tokens, moe_gain, route_ids, route_gates, gate_halves, up_halves, down_halves, head_gain, head_weight, query_scale, members, click_targets):
    device_count = N_DP * N_EXPERT
    route_total = TOK_DEV * TOPK
    normed = rms_scale(tokens.astype(jnp.float32), moe_gain).astype(jnp.bfloat16)
    flat_ids = route_ids.reshape(device_count, route_total).astype(jnp.int32)
    onehot = (flat_ids[:, :, None] == jnp.arange(EXPERTS, dtype=jnp.int32)[None, None, :]).astype(jnp.int32)
    earlier = jnp.cumsum(onehot, axis=1) - onehot
    slot_ids = lax.optimization_barrier(jnp.sum(earlier * onehot, axis=2)).astype(jnp.int32)
    device_ids = jnp.broadcast_to(jnp.arange(device_count, dtype=jnp.int32)[:, None], (device_count, route_total))
    token_ids = (device_ids * TOK_DEV + (jnp.arange(route_total, dtype=jnp.int32) // TOPK)[None, :]).astype(jnp.int32)
    slot_table = jnp.full((EXPERTS, device_count, CAP), TOKENS, jnp.int32).at[flat_ids, device_ids, slot_ids].set(token_ids)
    padded = jnp.concatenate([normed, jnp.zeros((1, D), jnp.bfloat16)], axis=0)

    def one_expert(expert_id):
        expert_rows = padded[slot_table[expert_id].reshape(-1)]
        summed = jnp.zeros((device_count * CAP, D), jnp.float32)
        for half_id in range(4):
            half_index = 4 * expert_id + half_id
            gate_part = lax.dynamic_index_in_dim(gate_halves, half_index, 0, keepdims=False)
            up_part = lax.dynamic_index_in_dim(up_halves, half_index, 0, keepdims=False)
            down_part = lax.dynamic_index_in_dim(down_halves, half_index, 0, keepdims=False)
            gate_out = jnp.dot(expert_rows, gate_part, preferred_element_type=jnp.float32)
            up_out = jnp.dot(expert_rows, up_part, preferred_element_type=jnp.float32)
            hidden = (jax.nn.silu(gate_out) * up_out).astype(jnp.bfloat16)
            partial_out = jnp.dot(hidden, down_part, preferred_element_type=jnp.float32).astype(jnp.bfloat16)
            summed = summed + partial_out.astype(jnp.float32)
        return summed.astype(jnp.bfloat16)
    outputs = lax.map(one_expert, jnp.arange(EXPERTS, dtype=jnp.int32))
    picked = outputs[flat_ids, device_ids * CAP + slot_ids].astype(jnp.float32).reshape(TOKENS, TOPK, D)
    layer_out = (tokens.astype(jnp.float32) + lax.optimization_barrier(jnp.sum(route_gates[:, :, None] * picked, axis=1))).astype(jnp.bfloat16)
    head_in = rms_scale(layer_out.astype(jnp.float32), head_gain).astype(jnp.bfloat16)
    embedding = jnp.dot(head_in, head_weight, preferred_element_type=jnp.float32).astype(jnp.bfloat16)
    grouped = embedding[members].astype(jnp.float32).reshape(SHOTS, PATCHES + QUERIES, DH)
    key_rows = grouped[:, :PATCHES]
    query_rows = grouped[:, PATCHES:] * query_scale
    click_logits = jnp.einsum('sqd,spd->sqp', query_rows, key_rows, precision=lax.Precision.HIGHEST) / math.sqrt(DH)
    log_total = jnp.log(lax.optimization_barrier(jnp.sum(jnp.exp(click_logits), axis=-1)))
    chosen_logit = jnp.take_along_axis(click_logits, click_targets[:, :, None], axis=-1)[:, :, 0]
    click_loss = log_total - chosen_logit
    return (layer_out, click_logits, click_loss)
```

```python
import functools
import math

import jax
import jax.numpy as jnp
from jax import lax
from jax.experimental import pallas as pl
from jax.experimental.pallas import tpu as pltpu
from jax.sharding import PartitionSpec as P

PATCHES = 56
QUERIES = 8


def rms_scale(values, gains):
    mean_square = jnp.mean(values * values, axis=-1, keepdims=True)
    return values * lax.rsqrt(mean_square + 1e-06) * gains


def expert_ffn(block_in, gate_part, up_part, down_part):
    block_shape = block_in.shape
    flat_rows = block_in.reshape(-1, block_shape[-1])
    gate_out = jnp.dot(flat_rows, gate_part, preferred_element_type=jnp.float32)
    up_out = jnp.dot(flat_rows, up_part, preferred_element_type=jnp.float32)
    hidden = (jax.nn.silu(gate_out) * up_out).astype(jnp.bfloat16)
    partial_out = jnp.dot(hidden, down_part, preferred_element_type=jnp.float32).astype(
        jnp.bfloat16
    )
    return partial_out.reshape(block_shape)


MESH = pl.DeviceIdType.MESH


def flip(value, bits, count):
    bit = 1
    while bit < count:
        if bits & bit:
            value = value + bit * (1 - 2 * ((value // bit) % 2))
        bit *= 2
    return value


def place(count, per_row):
    dp, column = lax.axis_index("dp"), lax.axis_index("expert")
    group, quarter = dp * per_row + column // 4, column % 4

    def across(offset):
        other = flip(group, offset, count)
        return (other // per_row, (other % per_row) * 4 + quarter)

    def beside(bits):
        return (dp, (column // 4) * 4 + flip(quarter, bits, 4))

    return group, quarter, across, beside


def greet(count, across, beside):
    barrier = pltpu.get_barrier_semaphore()
    for offset in range(1, count):
        pl.semaphore_signal(barrier, inc=1, device_id=across(offset), device_id_type=MESH)
    for bits in (1, 2):
        pl.semaphore_signal(barrier, inc=1, device_id=beside(bits), device_id_type=MESH)
    pl.semaphore_wait(barrier, count + 1)


def remote(source, target, send, receive, device):
    return pltpu.make_async_remote_copy(
        src_ref=source,
        dst_ref=target,
        send_sem=send,
        recv_sem=receive,
        device_id=device,
        device_id_type=MESH,
    )


def via(offset):
    return 1 + (offset // 2) % 2


def dispatch_kernel(count, per_row, block_ref, out_ref, own, s1, r1, s2, r2, s3, r3):
    group, quarter, across, beside = place(count, per_row)
    greet(count, across, beside)
    order = list(range(0, count, 2)) + list(range(1, count, 2))
    keep = pltpu.make_async_copy(block_ref.at[group], out_ref.at[quarter, group], own.at[0])
    started = []
    first = {}
    for offset in sorted(range(1, count), key=lambda o: bin(o).count("1")):
        first[offset] = remote(
            block_ref.at[flip(group, offset, count)],
            out_ref.at[quarter, group],
            s1.at[offset],
            r1.at[offset],
            across(offset),
        )
        first[offset].start()
        started.append(first[offset])
    keep.start()
    second = {}

    def relay(offset):
        bits = via(offset)
        second[bits, offset].wait_recv()
        held = out_ref.at[flip(quarter, bits, 4), flip(group, offset, count)]
        copy = remote(held, held, s3.at[offset], r3.at[offset], beside(3 - bits))
        copy.start()
        started.append(copy)
        return copy

    relays = []
    for place_in, offset in enumerate(order):
        slot = out_ref.at[quarter, flip(group, offset, count)]
        if offset:
            first[offset].wait_recv()
        for bits in (via(offset), 3 - via(offset)):
            second[bits, offset] = remote(
                slot if offset else block_ref.at[group],
                slot,
                s2.at[bits - 1, offset],
                r2.at[bits - 1, offset],
                beside(bits),
            )
            second[bits, offset].start()
            started.append(second[bits, offset])
        if place_in >= 2:
            relays.append(relay(order[place_in - 2]))
    for offset in order[-2:]:
        relays.append(relay(offset))
    for offset in order:
        second[3 - via(offset), offset].wait_recv()
    for copy in relays:
        copy.wait_recv()
    for copy in started:
        copy.wait_send()
    keep.wait()


def return_kernel(
    count, per_row, part_ref, out_ref, early, merged, late, total, own, s0, r0, s1, r1, s2, r2
):
    group, quarter, across, beside = place(count, per_row)
    greet(count, across, beside)
    order = list(range(1, count, 2)) + list(range(2, count, 2)) + [0]
    started = []
    opening, middle, closing = {}, {}, {}

    def at(bits, offset):
        return part_ref.at[flip(quarter, bits, 4), flip(group, offset, count)]

    def to_owner(bits, offset, source):
        middle[bits, offset] = remote(
            source,
            late.at[bits - 1, offset],
            s1.at[bits - 1, offset],
            r1.at[bits - 1, offset],
            beside(bits),
        )
        middle[bits, offset].start()
        started.append(middle[bits, offset])

    for offset in order:
        bits = via(offset)
        opening[offset] = remote(
            at(3, offset), early.at[offset], s0.at[offset], r0.at[offset], beside(bits)
        )
        opening[offset].start()
        started.append(opening[offset])
        to_owner(bits, offset, at(bits, offset))
    waiting = None
    for offset in order:
        opening[offset].wait_recv()
        bits = 3 - via(offset)
        merged[offset] = (
            at(bits, offset)[...].astype(jnp.float32) + early[offset].astype(jnp.float32)
        ).astype(jnp.bfloat16)
        if waiting is not None:
            to_owner(3 - via(waiting), waiting, merged.at[waiting])
        waiting = offset
    last_merged = waiting
    waiting = None

    def send_home(offset):
        closing[offset] = remote(
            total.at[offset], out_ref.at[group], s2.at[offset], r2.at[offset], across(offset)
        )
        closing[offset].start()
        started.append(closing[offset])

    to_owner(3 - via(last_merged), last_merged, merged.at[last_merged])
    for offset in order:
        for bits in (1, 2):
            middle[bits, offset].wait_recv()
        total[offset] = (
            at(0, offset)[...].astype(jnp.float32)
            + late[0, offset].astype(jnp.float32)
            + late[1, offset].astype(jnp.float32)
        ).astype(jnp.bfloat16)
        if waiting is not None:
            send_home(waiting)
        waiting = offset
    keep = pltpu.make_async_copy(total.at[0], out_ref.at[group], own.at[0])
    keep.start()
    for offset in order[:-1]:
        closing[offset].wait_recv()
    for copy in started:
        copy.wait_send()
    keep.wait()


def dispatch_rows(blocks, per_row):
    count, capacity, width = blocks.shape
    dma = pltpu.SemaphoreType.DMA
    return pl.pallas_call(
        functools.partial(dispatch_kernel, count, per_row),
        out_shape=jax.ShapeDtypeStruct((4, count, capacity, width), blocks.dtype),
        in_specs=[pl.BlockSpec(memory_space=pltpu.VMEM)],
        out_specs=pl.BlockSpec(memory_space=pl.ANY),
        scratch_shapes=[
            dma((1,)),
            dma((count,)),
            dma((count,)),
            dma((2, count)),
            dma((2, count)),
            dma((count,)),
            dma((count,)),
        ],
        compiler_params=pltpu.CompilerParams(collective_id=0, has_side_effects=True),
        name="dispatch_rows",
    )(blocks)


def return_rows(parts, per_row):
    _, count, capacity, width = parts.shape
    dma = pltpu.SemaphoreType.DMA
    block = (count, capacity, width)
    return pl.pallas_call(
        functools.partial(return_kernel, count, per_row),
        out_shape=jax.ShapeDtypeStruct(block, parts.dtype),
        in_specs=[pl.BlockSpec(memory_space=pltpu.VMEM)],
        out_specs=pl.BlockSpec(memory_space=pl.ANY),
        scratch_shapes=[
            pltpu.VMEM(block, parts.dtype),
            pltpu.VMEM(block, parts.dtype),
            pltpu.VMEM((2, *block), parts.dtype),
            pltpu.VMEM(block, parts.dtype),
            dma((1,)),
            dma((count,)),
            dma((count,)),
            dma((2, count)),
            dma((2, count)),
            dma((count,)),
            dma((count,)),
        ],
        compiler_params=pltpu.CompilerParams(collective_id=1, has_side_effects=True),
        name="return_rows",
    )(parts)


def shards(
    tokens,
    moe_gain,
    route_ids,
    route_gates,
    gate_halves,
    up_halves,
    down_halves,
    head_gain,
    head_weight,
    query_scale,
    members,
    click_targets,
):
    row_count = lax.axis_size("dp")
    col_count = lax.axis_size("expert")
    tok_count, model_width = tokens.shape
    route_count = route_ids.shape[1]
    expert_count = row_count * col_count // 4
    per_row = col_count // 4
    capacity = max(2, 5 * tok_count * route_count // (4 * expert_count))
    head_width = head_weight.shape[1]
    gate_part = gate_halves[0]
    up_part = up_halves[0]
    down_part = down_halves[0]
    normed = rms_scale(tokens.astype(jnp.float32), moe_gain).astype(jnp.bfloat16)
    flat_ids = route_ids.reshape(-1)
    onehot = (flat_ids[:, None] == jnp.arange(expert_count, dtype=jnp.int32)[None, :]).astype(
        jnp.int32
    )
    earlier = jnp.cumsum(onehot, axis=0) - onehot
    slot_ids = jnp.sum(earlier * onehot, axis=1)
    target = (flat_ids * capacity + slot_ids).reshape(tok_count, route_count)
    slots = jnp.arange(expert_count * capacity, dtype=jnp.int32)
    chosen = target.T[:, None, :] == slots[None, :, None]
    fill = jnp.any(chosen, axis=0).astype(jnp.bfloat16)
    dispatch = jnp.dot(fill, normed, preferred_element_type=jnp.float32).astype(jnp.bfloat16)
    arrived = dispatch_rows(dispatch.reshape(expert_count, capacity, model_width), per_row)
    partial_out = expert_ffn(arrived, gate_part, up_part, down_part)
    outputs = return_rows(partial_out, per_row).reshape(expert_count * capacity, model_width)
    mixed = jnp.zeros((tok_count, model_width), jnp.float32)
    for k in range(route_count):
        pick = (target[:, k, None] == slots[None, :]).astype(jnp.bfloat16)
        picked = jnp.dot(pick, outputs, preferred_element_type=jnp.float32)
        mixed = mixed + route_gates[:, k, None] * picked
    layer_out = (tokens.astype(jnp.float32) + mixed).astype(jnp.bfloat16)
    head_in = rms_scale(layer_out.astype(jnp.float32), head_gain).astype(jnp.bfloat16)
    embedding = jnp.dot(
        head_in,
        lax.all_gather(head_weight, "expert", axis=0, tiled=True),
        preferred_element_type=jnp.float32,
    ).astype(jnp.bfloat16)
    row_length = col_count * tok_count
    local_ids = members % row_length
    portion = lax.all_gather(embedding, "expert", axis=0, tiled=True)
    select = (local_ids[:, None] == jnp.arange(portion.shape[0], dtype=jnp.int32)[None, :]).astype(
        jnp.bfloat16
    )
    regrouped = jnp.dot(select, portion, preferred_element_type=jnp.float32)
    span_rows = PATCHES + QUERIES
    grouped = regrouped.reshape(tok_count // span_rows, span_rows, head_width)
    key_rows = grouped[:, :PATCHES]
    query_rows = grouped[:, PATCHES:] * query_scale
    click_logits = jnp.einsum(
        "sqd,spd->sqp", query_rows, key_rows, precision=lax.Precision.HIGHEST
    ) / math.sqrt(head_width)
    log_total = jnp.log(jnp.sum(jnp.exp(click_logits), axis=-1))
    chosen_logit = jnp.take_along_axis(click_logits, click_targets[:, :, None], axis=-1)[:, :, 0]
    click_loss = log_total - chosen_logit
    return (layer_out, click_logits, click_loss)


def solution(mesh):
    in_specs = (
        P(("dp", "expert"), None),
        P(),
        P(("dp", "expert"), None),
        P(("dp", "expert"), None),
        P(("dp", "expert"), None, None),
        P(("dp", "expert"), None, None),
        P(("dp", "expert"), None, None),
        P(),
        P("expert", None),
        P(),
        P(("dp", "expert")),
        P(("dp", "expert"), None),
    )
    out_specs = (
        P(("dp", "expert"), None),
        P(("dp", "expert"), None, None),
        P(("dp", "expert"), None),
    )
    return jax.shard_map(shards, mesh=mesh, in_specs=in_specs, out_specs=out_specs, check_vma=False)
```
